32 devices in a mesh: dp: 4 (over x, core), ctx: 2 (over y), tensor: 4 (over z).
Axes of the slice: x: 2, y: 2, z: 4, core: 2. Of those that a mesh axis runs over, the one named last changes fastest.
Arguments:
- tokens: bfloat16 [4, 1024, 768], P('dp', 'ctx'), may hold values from -24 to 24
- lengths: int32 [4], P('dp'), may hold values from 128 to 1024, as said below
- cotangent: bfloat16 [4, 1024, 768], P('dp', 'ctx'), may hold values from -6 to 6
- qkv_weight: bfloat16 [3, 768, 768], P(None, 'dp', 'tensor'), may hold values from -0.21875 to 0.21875
- query_bias: float32 [768], P('tensor'), may hold values from -3 to 3
- value_bias: float32 [768], P('tensor'), may hold values from -0.18 to 0.18
- proj_weight: bfloat16 [768, 768], P('tensor', 'dp'), may hold values from -6 to 6
- proj_bias: float32 [768], replicated, may hold values from -2 to 2
- first_gain: float32 [768], replicated, may hold values from 0.1 to 1.9
- first_shift: float32 [768], replicated, may hold values from -2 to 2
- up_weight: bfloat16 [768, 3072], P('dp', 'tensor'), may hold values from -0.21875 to 0.21875
- up_bias: float32 [3072], P('tensor'), may hold values from -2 to 2
- down_weight: bfloat16 [3072, 768], P('tensor', 'dp'), may hold values from -0.109375 to 0.109375
- down_bias: float32 [768], replicated, may hold values from -2 to 2
- second_gain: float32 [768], replicated, may hold values from 0.1 to 1.9
- second_shift: float32 [768], replicated, may hold values from -2 to 2
Outputs:
- output: bfloat16 [4, 1024, 768], P('dp', 'ctx')
- grad_tokens: float32 [4, 1024, 768], P('dp', 'ctx')
- grad_qkv: float32 [3, 768, 768], P(None, 'dp', 'tensor')
- grad_query_bias: float32 [768], P('tensor')
- grad_value_bias: float32 [768], P('tensor')
- grad_proj: float32 [768, 768], P('tensor', 'dp')
- grad_proj_bias: float32 [768], replicated
- grad_first_gain: float32 [768], replicated
- grad_first_shift: float32 [768], replicated
- grad_up: float32 [768, 3072], P('dp', 'tensor')
- grad_up_bias: float32 [3072], P('tensor')
- grad_down: float32 [3072, 768], P('tensor', 'dp')
- grad_down_bias: float32 [768], replicated
- grad_second_gain: float32 [768], replicated
- grad_second_shift: float32 [768], replicated
The draws below stay inside these ranges and needn't reach their ends.
Inputs may be any that keep to these rules, and one draw needn't show every extreme that they name: `lengths`: positions at or beyond a sequence's length are padding; they are still computed, but no position attends to them.
All inputs are finite; a program needn't handle non-finite values.
Results may differ from the reference program's by a relative error of at most 0.013.
The reference program's roundings to bfloat16 on the way count: a program that leaves them out, or rounds other values in their place, can miss the bound.
Values may be sent and summed in bfloat16 or wider, within the bound.
A program may use at most 128 MiB of HBM per device.

```python
import math
import jax
import jax.numpy as jnp
from jax import lax

D = 768
H = 12
HD = 64
FF = 3072
SEQS = 4
LEN = 1024


def draw_tokens(key, part):
    base = jax.random.normal(key, (SEQS, LEN, D), jnp.float32)
    return jnp.clip(base, -6.0, 6.0).astype(jnp.bfloat16)


def draw_lengths(key, part):
    first_key, second_key = jax.random.split(jax.random.fold_in(key, 7))
    drawn = jax.random.randint(first_key, (SEQS,), LEN // 8, LEN + 1, dtype=jnp.int32)
    chosen = jax.random.randint(second_key, (), 0, SEQS, dtype=jnp.int32)
    drawn = drawn.at[chosen].set(LEN)
    drawn = drawn.at[(chosen + 1) % SEQS].set(LEN // 8)
    return drawn.astype(jnp.int32)


def block_scale(own_key, dims, cuts, low, high):
    factor_of = 1.0
    for position, shards_of in cuts:
        draws = jax.random.uniform(jax.random.fold_in(jax.random.fold_in(own_key, 6), position), (shards_of,), jnp.float32, low / len(cuts), high / len(cuts))
        factor_of = factor_of * jnp.repeat(jnp.exp(draws), dims[position] // shards_of).reshape((-1,) + (1,) * (len(dims) - 1 - position))
    return factor_of


def normal_values(rng, dims, width, most, pieces=(), held_as=jnp.bfloat16):
    gain = block_scale(rng, dims, pieces, -0.22, 0.18) if pieces else 1.0
    values = jax.random.normal(rng, dims, jnp.float32) * width * gain
    return jnp.minimum(jnp.maximum(values, -most), most).astype(held_as)


def setup_inputs(seed: int = 0) -> dict:
    streams_of = jax.random.split(jax.random.key(seed), 17)
    tokens = draw_tokens(jax.random.fold_in(streams_of[16], 71), 0)
    lengths = draw_lengths(jax.random.fold_in(streams_of[16], 71), 0)
    cotangent = normal_values(streams_of[2], (SEQS, LEN, D), 1.0, 6.0, ((0, 4), (1, 2)))
    qkv_weight = normal_values(streams_of[3], (3, D, D), D ** -0.5, 0.21875, ((1, 4), (2, 4)))
    query_bias = normal_values(streams_of[4], (D,), 0.5, 3.0, ((0, 4),), jnp.float32)
    value_bias = normal_values(streams_of[5], (D,), 0.03, 0.18, ((0, 4),), jnp.float32)
    proj_weight = normal_values(streams_of[6], (D, D), (max(1, 2 * D // LEN)) ** -0.5, 6.0, ((0, 4), (1, 4)))
    proj_bias = normal_values(streams_of[7], (D,), 0.3, 2.0, (), jnp.float32)
    first_gain = jnp.clip(1.0 + 0.18 * jax.random.normal(streams_of[8], (D,), jnp.float32), 0.1, 1.9)
    first_shift = normal_values(streams_of[9], (D,), 0.3, 2.0, (), jnp.float32)
    up_weight = normal_values(streams_of[10], (D, FF), D ** -0.5, 0.21875, ((0, 4), (1, 4)))
    up_bias = normal_values(streams_of[11], (FF,), 0.3, 2.0, ((0, 4),), jnp.float32)
    down_weight = normal_values(streams_of[12], (FF, D), FF ** -0.5, 0.109375, ((0, 4), (1, 4)))
    down_bias = normal_values(streams_of[13], (D,), 0.3, 2.0, (), jnp.float32)
    second_gain = jnp.clip(1.0 + 0.18 * jax.random.normal(streams_of[14], (D,), jnp.float32), 0.1, 1.9)
    second_shift = normal_values(streams_of[15], (D,), 0.3, 2.0, (), jnp.float32)
    return dict(tokens=tokens, lengths=lengths, cotangent=cotangent, qkv_weight=qkv_weight, query_bias=query_bias, value_bias=value_bias, proj_weight=proj_weight, proj_bias=proj_bias, first_gain=first_gain, first_shift=first_shift, up_weight=up_weight, up_bias=up_bias, down_weight=down_weight, down_bias=down_bias, second_gain=second_gain, second_shift=second_shift)


EPSILON = 1e-05
NEGATIVE = -1e+30
ROOT_HALF = 0.7071067811865476
ROOT_TWO_PI = 2.5066282746310002
HIGHEST = lax.Precision.HIGHEST

def rounded(array):
    return lax.optimization_barrier(array.astype(jnp.bfloat16))

def layer_norm(hidden_in, norm_gain, norm_shift):
    centred = hidden_in - lax.optimization_barrier(jnp.mean(hidden_in, axis=-1, keepdims=True))
    inverse = lax.rsqrt(lax.optimization_barrier(jnp.mean(centred * centred, axis=-1, keepdims=True)) + EPSILON)
    normed = centred * inverse
    return (normed * norm_gain + norm_shift, normed, inverse)

def norm_back(upstream, normed, inverse, norm_gain):
    scaled = upstream * norm_gain
    return inverse * (scaled - lax.optimization_barrier(jnp.mean(scaled, axis=-1, keepdims=True)) - normed * lax.optimization_barrier(jnp.mean(scaled * normed, axis=-1, keepdims=True)))

def gelu_value(pre_act):
    return 0.5 * pre_act * (1.0 + jax.scipy.special.erf(pre_act * ROOT_HALF))

def gelu_slope(pre_act):
    return 0.5 * (1.0 + jax.scipy.special.erf(pre_act * ROOT_HALF)) + pre_act * jnp.exp(-0.5 * pre_act * pre_act) / ROOT_TWO_PI

def attend_forward(queries, key_rows, value_rows, key_valid):
    block_rows = math.gcd(LEN, 512)
    block_count = LEN // block_rows
    score_scale = 1.0 / math.sqrt(HD)
    key_float = key_rows.astype(jnp.float32)
    value_float = value_rows.astype(jnp.float32)
    key_mask = key_valid[None, None, :]

    def one_block(query_block):
        scores = jnp.einsum('qhe,khe->hqk', query_block, key_float, precision=HIGHEST) * score_scale
        scores = jnp.where(key_mask, scores, NEGATIVE)
        row_max = lax.optimization_barrier(jnp.max(scores, axis=-1))
        weights_now = jnp.where(key_mask, jnp.exp(scores - row_max[..., None]), 0.0)
        row_total = lax.optimization_barrier(jnp.sum(weights_now, axis=-1))
        weights_low = rounded(weights_now).astype(jnp.float32)
        mixed = jnp.einsum('hqk,khe->qhe', weights_low, value_float, precision=HIGHEST)
        return (mixed / row_total.T[..., None], row_max + jnp.log(row_total))
    query_blocks = queries.astype(jnp.float32).reshape(block_count, block_rows, H, HD)
    attended, totals = lax.map(one_block, query_blocks)
    log_total = totals.transpose(1, 0, 2).reshape(H, LEN)
    return (attended.reshape(LEN, H, HD), log_total)

def attend_backward(queries, key_rows, value_rows, key_valid, d_heads, attended, log_total):
    block_rows = math.gcd(LEN, 512)
    block_count = LEN // block_rows
    score_scale = 1.0 / math.sqrt(HD)
    key_float = key_rows.astype(jnp.float32)
    value_float = value_rows.astype(jnp.float32)
    key_mask = key_valid[None, None, :]
    head_float = d_heads.astype(jnp.float32)
    row_delta = lax.optimization_barrier(jnp.sum(head_float * attended, axis=-1))

    def one_block(running, block_item):
        key_total, value_total = running
        query_block, dhead_block, delta_block, total_block = block_item
        scores = jnp.einsum('qhe,khe->hqk', query_block, key_float, precision=HIGHEST) * score_scale
        scores = jnp.where(key_mask, scores, NEGATIVE)
        probabilities = jnp.where(key_mask, jnp.exp(scores - total_block[..., None]), 0.0)
        probs_low = rounded(probabilities).astype(jnp.float32)
        value_total = value_total + jnp.einsum('hqk,qhe->khe', probs_low, dhead_block, precision=HIGHEST)
        d_probs = jnp.einsum('qhe,khe->hqk', dhead_block, value_float, precision=HIGHEST)
        d_scores = rounded(probabilities * (d_probs - delta_block.T[..., None])).astype(jnp.float32)
        d_query = jnp.einsum('hqk,khe->qhe', d_scores, key_float, precision=HIGHEST) * score_scale
        key_total = key_total + jnp.einsum('hqk,qhe->khe', d_scores, query_block, precision=HIGHEST) * score_scale
        return ((key_total, value_total), d_query)
    block_items = (queries.astype(jnp.float32).reshape(block_count, block_rows, H, HD), head_float.reshape(block_count, block_rows, H, HD), row_delta.reshape(block_count, block_rows, H), log_total.reshape(H, block_count, block_rows).transpose(1, 0, 2))
    zero_rows = jnp.zeros((LEN, H, HD), jnp.float32)
    (key_total, value_total), d_query = lax.scan(one_block, (zero_rows, zero_rows), block_items)
    return (d_query.reshape(LEN, H, HD), key_total, value_total)

def sequence_pass(seq_tokens, seq_length, seq_cot, qkv_weight, query_bias, value_bias, proj_weight, proj_bias, first_gain, first_shift, up_weight, up_bias, down_weight, down_bias, second_gain, second_shift):
    tok_float = seq_tokens.astype(jnp.float32)
    projected = jnp.einsum('td,ide->ite', tok_float, qkv_weight.astype(jnp.float32), precision=HIGHEST)
    queries = rounded(projected[0] + query_bias).reshape(LEN, H, HD)
    key_rows = rounded(projected[1]).reshape(LEN, H, HD)
    value_rows = rounded(projected[2] + value_bias).reshape(LEN, H, HD)
    key_valid = jnp.arange(LEN, dtype=jnp.int32) < seq_length
    attended, log_total = attend_forward(queries, key_rows, value_rows, key_valid)
    attended_low = rounded(attended.reshape(LEN, D))
    first_sum = tok_float + jnp.dot(attended_low, proj_weight, preferred_element_type=jnp.float32) + proj_bias
    first_out, first_normed, first_inverse = layer_norm(first_sum, first_gain, first_shift)
    first_low = rounded(first_out)
    pre_act = jnp.dot(first_low, up_weight, preferred_element_type=jnp.float32) + up_bias
    hidden = rounded(gelu_value(pre_act))
    second_sum = first_out + jnp.dot(hidden, down_weight, preferred_element_type=jnp.float32) + down_bias
    result, second_normed, second_inverse = layer_norm(second_sum, second_gain, second_shift)
    output = result.astype(jnp.bfloat16)
    upstream = seq_cot.astype(jnp.float32)
    grad_second_shift = lax.optimization_barrier(jnp.sum(upstream, axis=0))
    grad_second_gain = lax.optimization_barrier(jnp.sum(upstream * second_normed, axis=0))
    d_second = norm_back(upstream, second_normed, second_inverse, second_gain)
    grad_down_bias = lax.optimization_barrier(jnp.sum(d_second, axis=0))
    d_second_low = rounded(d_second)
    grad_down = jnp.dot(hidden.T, d_second_low, preferred_element_type=jnp.float32)
    d_pre = jnp.dot(d_second_low, down_weight.T, preferred_element_type=jnp.float32) * gelu_slope(pre_act)
    grad_up_bias = lax.optimization_barrier(jnp.sum(d_pre, axis=0))
    d_pre_low = rounded(d_pre)
    grad_up = jnp.dot(first_low.T, d_pre_low, preferred_element_type=jnp.float32)
    d_first = jnp.dot(d_pre_low, up_weight.T, preferred_element_type=jnp.float32) + d_second
    grad_first_shift = lax.optimization_barrier(jnp.sum(d_first, axis=0))
    grad_first_gain = lax.optimization_barrier(jnp.sum(d_first * first_normed, axis=0))
    d_attn = norm_back(d_first, first_normed, first_inverse, first_gain)
    grad_proj_bias = lax.optimization_barrier(jnp.sum(d_attn, axis=0))
    d_attn_low = rounded(d_attn)
    grad_proj = jnp.dot(attended_low.T, d_attn_low, preferred_element_type=jnp.float32)
    d_heads = rounded(jnp.dot(d_attn_low, proj_weight.T, preferred_element_type=jnp.float32)).reshape(LEN, H, HD)
    d_queries, d_keys, d_values = attend_backward(queries, key_rows, value_rows, key_valid, d_heads, attended, log_total)
    grad_query_bias = lax.optimization_barrier(jnp.sum(d_queries.reshape(LEN, D), axis=0))
    grad_value_bias = lax.optimization_barrier(jnp.sum(d_values.reshape(LEN, D), axis=0))
    d_stack = jnp.stack([rounded(d_queries.reshape(LEN, D)), rounded(d_keys.reshape(LEN, D)), rounded(d_values.reshape(LEN, D))]).astype(jnp.float32)
    grad_qkv = jnp.einsum('td,ite->ide', tok_float, d_stack, precision=HIGHEST)
    grad_tokens = d_attn + jnp.einsum('ite,ide->td', d_stack, qkv_weight.astype(jnp.float32), precision=HIGHEST)
    grads = (grad_qkv, grad_query_bias, grad_value_bias, grad_proj, grad_proj_bias, grad_first_gain, grad_first_shift, grad_up, grad_up_bias, grad_down, grad_down_bias, grad_second_gain, grad_second_shift)
    return ((output, grad_tokens), grads)

def reference(tokens, lengths, cotangent, qkv_weight, query_bias, value_bias, proj_weight, proj_bias, first_gain, first_shift, up_weight, up_bias, down_weight, down_bias, second_gain, second_shift):
    params = (qkv_weight, query_bias, value_bias, proj_weight, proj_bias, first_gain, first_shift, up_weight, up_bias, down_weight, down_bias, second_gain, second_shift)

    def per_sequence(totals, seq_items):
        seq_tokens, seq_length, seq_cot = seq_items
        outputs, grads = sequence_pass(seq_tokens, seq_length, seq_cot, *params)
        totals = jax.tree.map(lambda total_part, new_part: total_part + new_part, totals, grads)
        return (totals, outputs)
    zero_grads = (jnp.zeros((3, D, D), jnp.float32), jnp.zeros((D,), jnp.float32), jnp.zeros((D,), jnp.float32), jnp.zeros((D, D), jnp.float32), jnp.zeros((D,), jnp.float32), jnp.zeros((D,), jnp.float32), jnp.zeros((D,), jnp.float32), jnp.zeros((D, FF), jnp.float32), jnp.zeros((FF,), jnp.float32), jnp.zeros((FF, D), jnp.float32), jnp.zeros((D,), jnp.float32), jnp.zeros((D,), jnp.float32), jnp.zeros((D,), jnp.float32))
    totals, outputs = lax.scan(per_sequence, zero_grads, (tokens, lengths, cotangent))
    output, grad_tokens = outputs
    return (output, grad_tokens, totals[0], totals[1], totals[2], totals[3], totals[4], totals[5], totals[6], totals[7], totals[8], totals[9], totals[10], totals[11], totals[12])
```

```python
import functools
import math

import jax
import jax.numpy as jnp
from jax import lax
from jax.experimental import pallas as pl
from jax.experimental.pallas import tpu as pltpu
from jax.sharding import PartitionSpec as P

HD = 64


EPSILON = 1e-05
NEGATIVE = -1e30
ROOT_HALF = 0.7071067811865476
ROOT_TWO_PI = 2.5066282746310002
MESH = pl.DeviceIdType.MESH
BF16 = jnp.bfloat16
F32 = jnp.float32
VMEM_SPEC = pl.BlockSpec(memory_space=pltpu.VMEM)
DMA = pltpu.SemaphoreType.DMA


def layer_norm(hidden_in, norm_gain, norm_shift):
    centred = hidden_in - jnp.mean(hidden_in, axis=-1, keepdims=True)
    inverse = lax.rsqrt(jnp.mean(centred * centred, axis=-1, keepdims=True) + EPSILON)
    normed = centred * inverse
    return (normed * norm_gain + norm_shift, normed, inverse)


def norm_back(upstream, normed, inverse, norm_gain):
    scaled = upstream * norm_gain
    return inverse * (
        scaled
        - jnp.mean(scaled, axis=-1, keepdims=True)
        - normed * jnp.mean(scaled * normed, axis=-1, keepdims=True)
    )


def gelu_value(pre_act):
    return 0.5 * pre_act * (1.0 + jax.scipy.special.erf(pre_act * ROOT_HALF))


def gelu_slope(pre_act):
    return (
        0.5 * (1.0 + jax.scipy.special.erf(pre_act * ROOT_HALF))
        + pre_act * jnp.exp(-0.5 * pre_act * pre_act) / ROOT_TWO_PI
    )


def peers_of(axis, size):
    me = lax.axis_index(axis)
    found = []
    for step in range(1, size):
        other = lax.rem(me + step, size)
        found.append((other, {axis: other}))
    return found


def grid_peers(sizes):
    count = sizes["dp"] * sizes["ctx"]
    me = lax.axis_index("dp") * sizes["ctx"] + lax.axis_index("ctx")
    found = []
    for step in range(1, count):
        other = lax.rem(me + step, count)
        found.append((other, {"dp": lax.div(other, sizes["ctx"]), "ctx": lax.rem(other, sizes["ctx"])}))
    return me, found


def greet(groups):
    barrier = pltpu.get_barrier_semaphore()
    total = 0
    for group in groups:
        for _, where in group:
            pl.semaphore_signal(barrier, inc=1, device_id=where, device_id_type=MESH)
            total += 1
    pl.semaphore_wait(barrier, total)


def send_all(pairs, peers, send_sem, recv_sem):
    copies = []
    for step, (other, where) in enumerate(peers):
        source, target = pairs(other)
        copies.append(
            pltpu.make_async_remote_copy(
                src_ref=source,
                dst_ref=target,
                send_sem=send_sem.at[step],
                recv_sem=recv_sem.at[step],
                device_id=where,
                device_id_type=MESH,
            )
        )
        copies[-1].start()
    return copies


def wait_all(copies):
    for copy in copies:
        copy.wait()


def slot_sum(slots, count):
    total = slots[0].astype(F32)
    for index in range(1, count):
        total = total + slots[index].astype(F32)
    return total


def sems(count):
    return [DMA((count,)), DMA((count,))]


def call(kernel, outs, scratch, collective_id, args, name, spec=None):
    return pl.pallas_call(
        kernel,
        out_shape=outs,
        in_specs=[VMEM_SPEC] * len(args),
        out_specs=[VMEM_SPEC] * len(outs),
        scratch_shapes=scratch,
        compiler_params=pltpu.CompilerParams(
            collective_id=collective_id, has_side_effects=True, vmem_limit_bytes=56 * 2**20
        ),
        name=name,
    )(*args)


def shaped(shape, dtype):
    return jax.ShapeDtypeStruct(shape, dtype)


def gather_kernel(sizes, qkv_ref, proj_ref, wide_qkv, wide_proj, *sem):
    me = lax.axis_index("dp")
    peers = peers_of("dp", sizes["dp"])
    greet([peers])
    first = send_all(lambda other: (qkv_ref, wide_qkv.at[:, me]), peers, sem[0], sem[1])
    second = send_all(lambda other: (proj_ref, wide_proj.at[me]), peers, sem[2], sem[3])
    wide_qkv[:, me] = qkv_ref[...]
    wide_proj[me] = proj_ref[...]
    wait_all(first)
    wait_all(second)


def ctx_gather_kernel(sizes, own_ref, wide, *sem):
    me = lax.axis_index("ctx")
    peers = peers_of("ctx", sizes["ctx"])
    greet([peers])
    copies = send_all(lambda other: (own_ref, wide.at[me]), peers, sem[0], sem[1])
    wide[me] = own_ref[...]
    wait_all(copies)


def ctx_sum_kernel(sizes, part_ref, total_ref, slots, *sem):
    me = lax.axis_index("ctx")
    peers = peers_of("ctx", sizes["ctx"])
    greet([peers])
    copies = send_all(lambda other: (part_ref.at[other], slots.at[me]), peers, sem[0], sem[1])
    slots[me] = part_ref[me]
    wait_all(copies)
    total_ref[...] = slot_sum(slots, sizes["ctx"])


def scatter_start(sizes, part_ref, slots, sem):
    me = lax.axis_index("tensor")
    peers = peers_of("tensor", sizes["tensor"])
    copies = send_all(lambda other: (part_ref.at[other], slots.at[me]), peers, sem[0], sem[1])
    slots[me] = part_ref[me]
    return copies


def spread_start(sizes, full_ref, value, sem):
    me = lax.axis_index("tensor")
    peers = peers_of("tensor", sizes["tensor"])
    full_ref[me] = value
    return send_all(lambda other: (full_ref.at[me], full_ref.at[me]), peers, sem[0], sem[1])


def first_kernel(
    sizes, part, tokens, bias, gain, shift, up, down,
    full, out_ref, normed_ref, inverse_ref, wide_up, wide_down,
    slots, *sem
):
    me = lax.axis_index("tensor")
    mine = lax.axis_index("dp")
    others = peers_of("dp", sizes["dp"])
    greet([peers_of("tensor", sizes["tensor"]), others])
    scatter = scatter_start(sizes, part, slots, sem[0:2])
    ups = send_all(lambda other: (up, wide_up.at[mine]), others, sem[4], sem[5])
    downs = send_all(lambda other: (down, wide_down.at[mine]), others, sem[6], sem[7])
    wide_up[mine] = up[...]
    wide_down[mine] = down[...]
    wait_all(scatter)
    first_sum = tokens[me].astype(F32) + slot_sum(slots, sizes["tensor"]) + bias[...]
    first_out, normed, inverse = layer_norm(first_sum, gain[...], shift[...])
    spread = spread_start(sizes, full, first_out.astype(BF16), sem[2:4])
    out_ref[...] = first_out
    normed_ref[...] = normed
    inverse_ref[...] = inverse
    wait_all(ups)
    wait_all(downs)
    wait_all(spread)


def second_kernel(
    sizes, part, first_out, cotangent, bias, gain, shift,
    full, output_ref, back_ref, vector_ref,
    slots, *sem
):
    me = lax.axis_index("tensor")
    greet([peers_of("tensor", sizes["tensor"])])
    scatter = scatter_start(sizes, part, slots, sem[0:2])
    wait_all(scatter)
    second_sum = first_out[...] + slot_sum(slots, sizes["tensor"]) + bias[...]
    result, normed, inverse = layer_norm(second_sum, gain[...], shift[...])
    upstream = cotangent[me].astype(F32)
    d_second = norm_back(upstream, normed, inverse, gain[...])
    spread = spread_start(sizes, full, d_second.astype(BF16), sem[2:4])
    output_ref[...] = result.astype(BF16)
    back_ref[...] = d_second
    vector_ref[0:1] = jnp.sum(upstream, axis=0, keepdims=True)
    vector_ref[1:2] = jnp.sum(upstream * normed, axis=0, keepdims=True)
    vector_ref[2:3] = jnp.sum(d_second, axis=0, keepdims=True)
    wait_all(spread)


def grads_start(sizes, grads, slots, sem):
    mine = lax.axis_index("dp")
    others = peers_of("dp", sizes["dp"])
    copies = send_all(lambda other: (grads.at[other], slots.at[mine]), others, sem[0], sem[1])
    slots[mine] = grads[mine]
    return copies


def grads_middle(sizes, copies, slots, blocks, sem):
    wait_all(copies)
    me = lax.axis_index("ctx")
    blocks[me] = slot_sum(slots, sizes["dp"]).astype(BF16)
    return send_all(
        lambda other: (blocks.at[me], blocks.at[me]), peers_of("ctx", sizes["ctx"]), sem[0], sem[1]
    )


def third_kernel(
    sizes, part, d_second, normed_ref, inverse_ref, gain, grads_a, grads_b,
    full, back_ref, vector_ref, owned_a, owned_b,
    slots, slots_a, slots_b, blocks_a, blocks_b, *sem
):
    greet(
        [
            peers_of("tensor", sizes["tensor"]),
            peers_of("dp", sizes["dp"]),
            peers_of("ctx", sizes["ctx"]),
        ]
    )
    scatter = scatter_start(sizes, part, slots, sem[0:2])
    moving_a = grads_start(sizes, grads_a, slots_a, sem[4:6])
    moving_b = grads_start(sizes, grads_b, slots_b, sem[6:8])
    wait_all(scatter)
    d_first = slot_sum(slots, sizes["tensor"]) + d_second[...]
    normed = normed_ref[...]
    d_attn = norm_back(d_first, normed, inverse_ref[...], gain[...])
    spread = spread_start(sizes, full, d_attn.astype(BF16), sem[2:4])
    back_ref[...] = d_attn
    vector_ref[0:1] = jnp.sum(d_first, axis=0, keepdims=True)
    vector_ref[1:2] = jnp.sum(d_first * normed, axis=0, keepdims=True)
    vector_ref[2:3] = jnp.sum(d_attn, axis=0, keepdims=True)
    moving_a = grads_middle(sizes, moving_a, slots_a, blocks_a, sem[8:10])
    moving_b = grads_middle(sizes, moving_b, slots_b, blocks_b, sem[10:12])
    wait_all(moving_a)
    owned_a[...] = slot_sum(blocks_a, sizes["ctx"])
    wait_all(moving_b)
    owned_b[...] = slot_sum(blocks_b, sizes["ctx"])
    wait_all(spread)


def last_kernel(
    sizes, part, d_attn, grads, vectors,
    full, owned, vector_ref,
    slots, slots_g, blocks, slots_v, grid_v, *sem
):
    me = lax.axis_index("tensor")
    rows = peers_of("tensor", sizes["tensor"])
    here, everyone = grid_peers(sizes)
    greet([rows, everyone])
    small = send_all(lambda other: (vectors, slots_v.at[me]), rows, sem[8], sem[9])
    slots_v[me] = vectors[...]
    scatter = scatter_start(sizes, part, slots, sem[0:2])
    moving = grads_start(sizes, grads, slots_g, sem[4:6])
    wait_all(small)
    own = vectors[...]
    row_ids = lax.broadcasted_iota(jnp.int32, own.shape, 0)
    grid_v[here] = jnp.where(row_ids < 6, slot_sum(slots_v, sizes["tensor"]), own)
    small = send_all(lambda other: (grid_v.at[here], grid_v.at[here]), everyone, sem[10], sem[11])
    wait_all(scatter)
    d_tokens = slot_sum(slots, sizes["tensor"]) + d_attn[...]
    spread = spread_start(sizes, full, d_tokens.astype(BF16), sem[2:4])
    moving = grads_middle(sizes, moving, slots_g, blocks, sem[6:8])
    wait_all(small)
    vector_ref[...] = slot_sum(grid_v, sizes["dp"] * sizes["ctx"])
    wait_all(moving)
    owned[...] = slot_sum(blocks, sizes["ctx"])
    wait_all(spread)


CONTRACT_LAST = (((1,), (1,)), ((), ()))
CONTRACT_FIRST = (((0,), (0,)), ((), ()))


def forward_kernel(score_scale, length_ref, q_ref, k_ref, v_ref, out_ref, low_ref, log_ref):
    length = length_ref[0]
    rows, width = q_ref.shape
    keys = k_ref.shape[0]
    block = math.gcd(rows, 256)
    valid = lax.broadcasted_iota(jnp.int32, (block, keys), 1) < length

    @pl.loop(0, rows // block)
    def _(step):
        here = pl.ds(pl.multiple_of(step * block, block), block)
        for head in range(width // HD):
            lanes = slice(head * HD, (head + 1) * HD)
            scores = lax.dot_general(
                q_ref[here, lanes], k_ref[:, lanes], CONTRACT_LAST, preferred_element_type=F32
            ) * score_scale
            scores = jnp.where(valid, scores, NEGATIVE)
            top = jnp.max(scores, axis=-1, keepdims=True)
            weights = jnp.where(valid, jnp.exp(scores - top), 0.0)
            total = jnp.sum(weights, axis=-1, keepdims=True)
            acc = jnp.dot(weights.astype(BF16), v_ref[:, lanes], preferred_element_type=F32)
            attended = acc / total
            out_ref[here, lanes] = attended
            low_ref[here, lanes] = attended.astype(BF16)
            log_ref[here, head : head + 1] = top + jnp.log(total)


def backward_kernel(
    score_scale, length_ref, q_ref, k_ref, v_ref, heads_ref, attended_ref, log_ref,
    dq_ref, dk_ref, dv_ref
):
    length = length_ref[0]
    rows, width = q_ref.shape
    keys = k_ref.shape[0]
    block = math.gcd(rows, 256)
    valid = lax.broadcasted_iota(jnp.int32, (block, keys), 1) < length
    dk_ref[...] = jnp.zeros_like(dk_ref)
    dv_ref[...] = jnp.zeros_like(dv_ref)

    @pl.loop(0, rows // block)
    def _(step):
        here = pl.ds(pl.multiple_of(step * block, block), block)
        for head in range(width // HD):
            lanes = slice(head * HD, (head + 1) * HD)
            q, k, v, d_heads = q_ref[here, lanes], k_ref[:, lanes], v_ref[:, lanes], heads_ref[here, lanes]
            delta = jnp.sum(d_heads.astype(F32) * attended_ref[here, lanes], axis=-1, keepdims=True)
            scores = lax.dot_general(q, k, CONTRACT_LAST, preferred_element_type=F32) * score_scale
            scores = jnp.where(valid, scores, NEGATIVE)
            probs = jnp.where(valid, jnp.exp(scores - log_ref[here, head : head + 1]), 0.0)
            d_probs = lax.dot_general(d_heads, v, CONTRACT_LAST, preferred_element_type=F32)
            d_scores = (probs * (d_probs - delta)).astype(BF16)
            dv_ref[:, lanes] += lax.dot_general(
                probs.astype(BF16), d_heads, CONTRACT_FIRST, preferred_element_type=F32
            )
            dk_ref[:, lanes] += lax.dot_general(
                d_scores, q, CONTRACT_FIRST, preferred_element_type=F32
            ) * score_scale
            dq_ref[here, lanes] = jnp.dot(d_scores, k, preferred_element_type=F32) * score_scale


def attention_call(kernel, outs, args, name):
    return pl.pallas_call(
        kernel,
        out_shape=outs,
        in_specs=[pl.BlockSpec(memory_space=pltpu.SMEM)] + [VMEM_SPEC] * (len(args) - 1),
        out_specs=[VMEM_SPEC] * len(outs),
        compiler_params=pltpu.CompilerParams(vmem_limit_bytes=56 * 2**20),
        name=name,
    )(*args)


def per_device(
    sizes,
    tokens,
    lengths,
    cotangent,
    qkv_weight,
    query_bias,
    value_bias,
    proj_weight,
    proj_bias,
    first_gain,
    first_shift,
    up_weight,
    up_bias,
    down_weight,
    down_bias,
    second_gain,
    second_shift,
):
    data, blocks, ranks = sizes["dp"], sizes["ctx"], sizes["tensor"]
    rows_in = tokens[0]
    row_count, model = rows_in.shape
    part_rows = row_count // ranks
    piece, local_width = qkv_weight.shape[1:]
    up_width = up_weight.shape[1]
    score_scale = 1.0 / math.sqrt(HD)
    split = (ranks, part_rows, model)
    part_slots = pltpu.VMEM(split, BF16)
    local = shaped((part_rows, model), F32)
    row = lambda vector: vector[None]

    wide_qkv, wide_proj = call(
        functools.partial(gather_kernel, sizes),
        [shaped((3, data, piece, local_width), BF16), shaped((data,) + proj_weight.shape, BF16)],
        sems(data - 1) * 2,
        0,
        (qkv_weight, proj_weight),
        "gather_weights",
    )
    wide_qkv = wide_qkv.reshape(3, model, local_width)
    wide_proj = wide_proj.transpose(1, 0, 2).reshape(local_width, model)

    projected = jnp.einsum("td,ide->ite", rows_in, wide_qkv, preferred_element_type=F32)
    queries = (projected[0] + query_bias).astype(BF16)
    own_kv = jnp.concatenate(
        [projected[1].astype(BF16), (projected[2] + value_bias).astype(BF16)], axis=1
    )
    (kv,) = call(
        functools.partial(ctx_gather_kernel, sizes),
        [shaped((blocks,) + own_kv.shape, BF16)],
        sems(blocks - 1),
        1,
        (own_kv,),
        "gather_keys",
    )
    kv = kv.reshape(blocks * row_count, 2 * local_width)
    keys, values = kv[:, :local_width], kv[:, local_width:]
    attended, attended_low, log_total = attention_call(
        functools.partial(forward_kernel, score_scale),
        [
            shaped((row_count, local_width), F32),
            shaped((row_count, local_width), BF16),
            shaped((row_count, local_width // HD), F32),
        ],
        (lengths, queries, keys, values),
        "attention_forward",
    )
    attn_part = jnp.dot(attended_low, wide_proj, preferred_element_type=F32).astype(BF16)

    first_low, first_out, first_normed, first_inverse, wide_up, wide_down = call(
        functools.partial(first_kernel, sizes),
        [
            shaped(split, BF16),
            local,
            local,
            shaped((part_rows, 1), F32),
            shaped((data,) + up_weight.shape, BF16),
            shaped((data,) + down_weight.shape, BF16),
        ],
        [part_slots] + sems(ranks - 1) * 2 + sems(data - 1) * 2,
        2,
        (
            attn_part.reshape(split),
            rows_in.reshape(split),
            row(proj_bias),
            row(first_gain),
            row(first_shift),
            up_weight,
            down_weight,
        ),
        "first_norm",
    )
    first_low = first_low.reshape(row_count, model)
    wide_up = wide_up.reshape(model, up_width)
    wide_down = wide_down.transpose(1, 0, 2).reshape(up_width, model)

    pre_act = jnp.dot(first_low, wide_up, preferred_element_type=F32) + up_bias
    hidden = gelu_value(pre_act).astype(BF16)
    down_part = jnp.dot(hidden, wide_down, preferred_element_type=F32).astype(BF16)
    d_second_low, output_part, d_second, second_vectors = call(
        functools.partial(second_kernel, sizes),
        [shaped(split, BF16), shaped((part_rows, model), BF16), local, shaped((3, model), F32)],
        [part_slots] + sems(ranks - 1) * 2,
        3,
        (
            down_part.reshape(split),
            first_out,
            cotangent[0].reshape(split),
            row(down_bias),
            row(second_gain),
            row(second_shift),
        ),
        "second_norm",
    )
    output = lax.all_gather(output_part, "tensor", axis=0, tiled=True)[None]
    d_second_low = d_second_low.reshape(row_count, model)
    grad_down = jnp.einsum("td,tf->df", d_second_low, hidden, preferred_element_type=F32)
    d_hidden = jnp.einsum("td,fd->tf", d_second_low, wide_down, preferred_element_type=F32)
    d_pre = d_hidden * gelu_slope(pre_act)
    grad_up_bias = jnp.sum(d_pre, axis=0)
    d_pre_low = d_pre.astype(BF16)
    grad_up = jnp.einsum("td,tf->df", first_low, d_pre_low, preferred_element_type=F32)
    first_part = jnp.einsum("tf,df->td", d_pre_low, wide_up, preferred_element_type=F32).astype(BF16)

    grad_shape = (data, model // data, up_width)
    grad_slots = pltpu.VMEM(grad_shape, BF16)
    ctx_slots = pltpu.VMEM((blocks,) + grad_shape[1:], BF16)
    d_attn_low, d_attn, first_vectors, own_up, own_down = call(
        functools.partial(third_kernel, sizes),
        [shaped(split, BF16), local, shaped((3, model), F32)] + [shaped(grad_shape[1:], F32)] * 2,
        [part_slots, grad_slots, grad_slots, ctx_slots, ctx_slots]
        + sems(ranks - 1) * 2
        + sems(data - 1) * 2
        + sems(blocks - 1) * 2,
        4,
        (
            first_part.reshape(split),
            d_second,
            first_normed,
            first_inverse,
            row(first_gain),
            grad_up.astype(BF16).reshape(grad_shape),
            grad_down.astype(BF16).reshape(grad_shape),
        ),
        "first_norm_back",
    )
    d_attn_low = d_attn_low.reshape(row_count, model)
    d_heads = jnp.einsum("td,ed->te", d_attn_low, wide_proj, preferred_element_type=F32).astype(BF16)
    d_query, key_grads, value_grads = attention_call(
        functools.partial(backward_kernel, score_scale),
        [shaped((row_count, local_width), F32)]
        + [shaped((blocks * row_count, local_width), F32)] * 2,
        (lengths, queries, keys, values, d_heads, attended, log_total),
        "attention_backward",
    )
    kv_part = jnp.concatenate([key_grads.astype(BF16), value_grads.astype(BF16)], axis=1)
    kv_shape = (blocks, row_count, 2 * local_width)
    (own_grads,) = call(
        functools.partial(ctx_sum_kernel, sizes),
        [shaped(kv_shape[1:], F32)],
        [pltpu.VMEM(kv_shape, BF16)] + sems(blocks - 1),
        5,
        (kv_part.reshape(kv_shape),),
        "sum_keys",
    )
    grad_query_bias = jnp.sum(d_query, axis=0)
    grad_value_bias = jnp.sum(own_grads[:, local_width:], axis=0)
    d_stack = jnp.concatenate([d_query.astype(BF16), own_grads.astype(BF16)], axis=1)
    grad_qkv = jnp.einsum("td,te->de", rows_in, d_stack, preferred_element_type=F32)
    grad_proj = jnp.einsum("td,te->de", d_attn_low, attended_low, preferred_element_type=F32)
    flat_qkv = wide_qkv.transpose(1, 0, 2).reshape(model, 3 * local_width)
    input_part = jnp.einsum("te,de->td", d_stack, flat_qkv, preferred_element_type=F32).astype(BF16)

    last_shape = (data, model // data, 4 * local_width)
    last_grads = jnp.concatenate([grad_qkv.astype(BF16), grad_proj.astype(BF16)], axis=1)
    vector_width = max(model, up_width, 2 * local_width)
    pad = lambda array: jnp.pad(array, ((0, 0), (0, vector_width - array.shape[1])))
    vectors = jnp.concatenate(
        [
            pad(second_vectors),
            pad(first_vectors),
            pad(grad_up_bias[None]),
            pad(jnp.concatenate([grad_query_bias, grad_value_bias])[None]),
        ]
    )
    grad_tokens, own_last, sums = call(
        functools.partial(last_kernel, sizes),
        [shaped(split, BF16), shaped(last_shape[1:], F32), shaped(vectors.shape, F32)],
        [
            part_slots,
            pltpu.VMEM(last_shape, BF16),
            pltpu.VMEM((blocks,) + last_shape[1:], BF16),
            pltpu.VMEM((ranks,) + vectors.shape, F32),
            pltpu.VMEM((data * blocks,) + vectors.shape, F32),
        ]
        + sems(ranks - 1) * 2
        + sems(data - 1)
        + sems(blocks - 1)
        + sems(ranks - 1)
        + sems(data * blocks - 1),
        6,
        (input_part.reshape(split), d_attn, last_grads.reshape(last_shape), vectors),
        "token_grads",
    )
    grad_tokens = grad_tokens.reshape(1, row_count, model).astype(F32)
    own_qkv = own_last[:, : 3 * local_width].reshape(-1, 3, local_width).transpose(1, 0, 2)
    return (
        output,
        grad_tokens,
        own_qkv,
        sums[7, :local_width],
        sums[7, local_width : 2 * local_width],
        own_last[:, 3 * local_width :].T,
        sums[5, :model],
        sums[4, :model],
        sums[3, :model],
        own_up,
        sums[6, :up_width],
        own_down.T,
        sums[2, :model],
        sums[1, :model],
        sums[0, :model],
    )


def solution(mesh):
    placed = (
        P("dp", "ctx", None),
        P("dp"),
        P("dp", "ctx", None),
        P(None, "dp", "tensor"),
        P("tensor"),
        P("tensor"),
        P("tensor", "dp"),
        P(),
        P(),
        P(),
        P("dp", "tensor"),
        P("tensor"),
        P("tensor", "dp"),
        P(),
        P(),
        P(),
    )
    return jax.shard_map(
        functools.partial(per_device, dict(mesh.shape)),
        mesh=mesh,
        in_specs=placed,
        out_specs=(
            P("dp", "ctx", None),
            P("dp", "ctx", None),
            P(None, "dp", "tensor"),
            P("tensor"),
            P("tensor"),
            P("tensor", "dp"),
            P(),
            P(),
            P(),
            P("dp", "tensor"),
            P("tensor"),
            P("tensor", "dp"),
            P(),
            P(),
            P(),
        ),
        check_vma=False,
    )
```

```python
import functools
import math

import jax
import jax.numpy as jnp
from jax import lax
from jax.experimental import pallas as pl
from jax.experimental.pallas import tpu as pltpu
from jax.sharding import PartitionSpec as P

HD = 64


EPSILON = 1e-05
NEGATIVE = -1e30
ROOT_HALF = 0.7071067811865476
ROOT_TWO_PI = 2.5066282746310002
MESH = pl.DeviceIdType.MESH
BF16 = jnp.bfloat16
F32 = jnp.float32
VMEM_SPEC = pl.BlockSpec(memory_space=pltpu.VMEM)
DMA = pltpu.SemaphoreType.DMA


def layer_norm(hidden_in, norm_gain, norm_shift):
    centred = hidden_in - jnp.mean(hidden_in, axis=-1, keepdims=True)
    inverse = lax.rsqrt(jnp.mean(centred * centred, axis=-1, keepdims=True) + EPSILON)
    normed = centred * inverse
    return (normed * norm_gain + norm_shift, normed, inverse)


def norm_back(upstream, normed, inverse, norm_gain):
    scaled = upstream * norm_gain
    return inverse * (
        scaled
        - jnp.mean(scaled, axis=-1, keepdims=True)
        - normed * jnp.mean(scaled * normed, axis=-1, keepdims=True)
    )


def gelu_value(pre_act):
    return 0.5 * pre_act * (1.0 + jax.scipy.special.erf(pre_act * ROOT_HALF))


def gelu_slope(pre_act):
    return (
        0.5 * (1.0 + jax.scipy.special.erf(pre_act * ROOT_HALF))
        + pre_act * jnp.exp(-0.5 * pre_act * pre_act) / ROOT_TWO_PI
    )


def peers_of(axis, size):
    me = lax.axis_index(axis)
    found = []
    for step in range(1, size):
        other = lax.rem(me + step, size)
        found.append((other, {axis: other}))
    return found


def grid_peers(sizes):
    count = sizes["dp"] * sizes["ctx"]
    me = lax.axis_index("dp") * sizes["ctx"] + lax.axis_index("ctx")
    found = []
    for step in range(1, count):
        other = lax.rem(me + step, count)
        found.append((other, {"dp": lax.div(other, sizes["ctx"]), "ctx": lax.rem(other, sizes["ctx"])}))
    return me, found


def greet(groups):
    barrier = pltpu.get_barrier_semaphore()
    total = 0
    for group in groups:
        for _, where in group:
            pl.semaphore_signal(barrier, inc=1, device_id=where, device_id_type=MESH)
            total += 1
    pl.semaphore_wait(barrier, total)


def send_all(pairs, peers, send_sem, recv_sem):
    copies = []
    for step, (other, where) in enumerate(peers):
        source, target = pairs(other)
        copies.append(
            pltpu.make_async_remote_copy(
                src_ref=source,
                dst_ref=target,
                send_sem=send_sem.at[step],
                recv_sem=recv_sem.at[step],
                device_id=where,
                device_id_type=MESH,
            )
        )
        copies[-1].start()
    return copies


def wait_all(copies):
    for copy in copies:
        copy.wait()


def slot_sum(slots, count):
    total = slots[0].astype(F32)
    for index in range(1, count):
        total = total + slots[index].astype(F32)
    return total


def sems(count):
    return [DMA((count,)), DMA((count,))]


def call(kernel, outs, scratch, collective_id, args, name, spec=None):
    return pl.pallas_call(
        kernel,
        out_shape=outs,
        in_specs=[VMEM_SPEC] * len(args),
        out_specs=[VMEM_SPEC] * len(outs),
        scratch_shapes=scratch,
        compiler_params=pltpu.CompilerParams(
            collective_id=collective_id, has_side_effects=True, vmem_limit_bytes=56 * 2**20
        ),
        name=name,
    )(*args)


def shaped(shape, dtype):
    return jax.ShapeDtypeStruct(shape, dtype)


def pair_roles(size):
    me = lax.axis_index("dp")
    partner = me + 1 - 2 * lax.rem(me, 2)
    far = [(lax.rem(me + 2 * step, size), lax.rem(me + size - 2 * step, size)) for step in range(1, size // 2)]
    return me, partner, far


def pair_group(size):
    me, partner, far = pair_roles(size)
    return [(partner, {"dp": partner})] + [(to, {"dp": to}) for to, _ in far]


def remote(source, target, send, recv, where):
    return pltpu.make_async_remote_copy(
        src_ref=source, dst_ref=target, send_sem=send, recv_sem=recv, device_id=where, device_id_type=MESH
    )


def pair_sems(size):
    return sems(1) + sems(max(1, size // 2 - 1)) * 2


def gather_start(size, own_ref, place, sem):
    me, partner, far = pair_roles(size)
    near = remote(own_ref, place(me), sem[0].at[0], sem[1].at[0], {"dp": partner})
    wide = [
        remote(own_ref, place(me), sem[2].at[step], sem[3].at[step], {"dp": to})
        for step, (to, _) in enumerate(far)
    ]
    for copy in wide + [near]:
        copy.start()
    return near, wide


def gather_pass(size, copies, place, sem):
    me, partner, far = pair_roles(size)
    passed = []
    for step, (_, origin) in enumerate(far):
        copies[1][step].wait()
        passed.append(
            remote(place(origin), place(origin), sem[4].at[step], sem[5].at[step], {"dp": partner})
        )
        passed[-1].start()
    return [copies[0]] + passed


def gather_kernel(sizes, qkv_ref, wide_qkv, *sem):
    size = sizes["dp"]
    greet([pair_group(size)])
    place = lambda index: wide_qkv.at[:, index]
    copies = gather_start(size, qkv_ref, place, sem)
    wide_qkv[:, lax.axis_index("dp")] = qkv_ref[...]
    wait_all(gather_pass(size, copies, place, sem))


def ctx_gather_kernel(sizes, own_ref, proj_ref, wide, wide_proj, *sem):
    me = lax.axis_index("ctx")
    size = sizes["dp"]
    peers = peers_of("ctx", sizes["ctx"])
    greet([peers, pair_group(size)])
    copies = send_all(lambda other: (own_ref, wide.at[me]), peers, sem[0], sem[1])
    place = lambda index: wide_proj.at[index]
    projs = gather_start(size, proj_ref, place, sem[2:])
    wide[me] = own_ref[...]
    wide_proj[lax.axis_index("dp")] = proj_ref[...]
    wait_all(gather_pass(size, projs, place, sem[2:]))
    wait_all(copies)


LAG = 2


def line_roles(size):
    me = lax.axis_index("tensor")
    lower, upper = lax.rem(me + size - 1, size), lax.rem(me + 1, size)
    return [(me, lower, upper), (size - 1 - me, upper, lower)]


def greet_line(size, groups):
    me = lax.axis_index("tensor")
    barrier = pltpu.get_barrier_semaphore()

    @pl.when(me > 0)
    def _():
        pl.semaphore_signal(barrier, inc=1, device_id={"tensor": me - 1}, device_id_type=MESH)

    @pl.when(me < size - 1)
    def _():
        pl.semaphore_signal(barrier, inc=1, device_id={"tensor": me + 1}, device_id_type=MESH)

    total = 0
    for group in groups:
        for _, where in group:
            pl.semaphore_signal(barrier, inc=1, device_id=where, device_id_type=MESH)
            total += 1

    beside = jnp.where(me > 0, 1, 0) + jnp.where(me < size - 1, 1, 0)
    pl.semaphore_wait(barrier, total + beside)


def both(*conditions):
    return functools.reduce(jnp.logical_and, conditions)


def line_start(size, part, slots, sem):
    count = part.shape[1]
    for flow, (place, toward, _) in enumerate(line_roles(size)):

        @pl.when(place == size - 1)
        def _(flow=flow, toward=toward):
            @pl.loop(0, count)
            def _(k):
                remote(
                    part.at[flow, k], slots.at[flow, k], sem[0].at[flow, k], sem[1].at[flow, k], {"tensor": toward}
                ).start()


def line_run(size, part, slots, sums, full, sem, finish):
    count = part.shape[1]
    roles = line_roles(size)

    def reduce_copy(flow, k, source):
        return remote(
            source.at[flow, k], slots.at[flow, k], sem[0].at[flow, k], sem[1].at[flow, k], {"tensor": roles[flow][1]}
        )

    def spread_copy(flow, k):
        return remote(
            full.at[flow, k], full.at[flow, k], sem[2].at[flow, k], sem[3].at[flow, k], {"tensor": roles[flow][2]}
        )

    @pl.loop(0, count + 2 * LAG * (size - 1))
    def _(step):
        for flow, (place, _, _) in enumerate(roles):
            k = step - LAG * (size - 1 - place)
            inside = both(k >= 0, k < count)

            @pl.when(both(inside, place > 0, place < size - 1))
            def _(flow=flow, k=k):
                reduce_copy(flow, k, sums).wait_recv()
                sums[flow, k] = (slots[flow, k].astype(F32) + part[flow, k].astype(F32)).astype(BF16)
                reduce_copy(flow, k, sums).start()

            @pl.when(both(inside, place == 0))
            def _(flow=flow, k=k):
                reduce_copy(flow, k, sums).wait_recv()
                full[flow, k] = finish(flow, k, slots[flow, k].astype(F32) + part[flow, k].astype(F32))
                spread_copy(flow, k).start()

        for flow, (place, _, _) in enumerate(roles):
            k = step - LAG * (size - 1) - LAG * place
            inside = both(k >= 0, k < count, place > 0)

            @pl.when(inside)
            def _(flow=flow, k=k):
                spread_copy(flow, k).wait_recv()

            @pl.when(both(inside, place < size - 1))
            def _(flow=flow, k=k):
                spread_copy(flow, k).start()

    for flow, (place, _, _) in enumerate(roles):

        @pl.when(place > 0)
        def _(flow=flow):
            @pl.loop(0, count)
            def _(k):
                reduce_copy(flow, k, sums).wait_send()

        @pl.when(place < size - 1)
        def _(flow=flow):
            @pl.loop(0, count)
            def _(k):
                spread_copy(flow, k).wait_send()


def spread_start(size, mine, full, sem):
    for flow, (place, _, away) in enumerate(line_roles(size)):

        @pl.when(place == 0)
        def _(flow=flow, away=away):
            @pl.loop(0, mine.shape[0])
            def _(k):
                remote(
                    mine.at[k], full.at[flow, k], sem[0].at[flow, k], sem[1].at[flow, k], {"tensor": away}
                ).start()
                full[flow, k] = mine[k]


def spread_run(size, mine, full, sem):
    count = mine.shape[0]
    roles = line_roles(size)

    def pass_on(flow, k):
        return remote(
            full.at[flow, k], full.at[flow, k], sem[0].at[flow, k], sem[1].at[flow, k], {"tensor": roles[flow][2]}
        )

    @pl.loop(0, count + LAG * (size - 1))
    def _(step):
        for flow, (place, _, _) in enumerate(roles):
            k = step - LAG * place
            inside = both(k >= 0, k < count, place > 0)

            @pl.when(inside)
            def _(flow=flow, k=k):
                pass_on(flow, k).wait_recv()

            @pl.when(both(inside, place < size - 1))
            def _(flow=flow, k=k):
                pass_on(flow, k).start()

    for flow, (place, _, _) in enumerate(roles):

        @pl.when(place < size - 1)
        def _(flow=flow):
            @pl.loop(0, count)
            def _(k):
                pass_on(flow, k).wait_send()


def line_sems(count, kinds):
    return [DMA((2, count))] * kinds


def ctx_sum_kernel(sizes, part_ref, mine, total_ref, full, slots, *sem):
    me = lax.axis_index("ctx")
    size = sizes["tensor"]
    peers = peers_of("ctx", sizes["ctx"])
    greet_line(size, [peers])
    copies = send_all(lambda other: (part_ref.at[other], slots.at[me]), peers, sem[0], sem[1])
    spread_start(size, mine, full, sem[2:4])
    slots[me] = part_ref[me]
    spread_run(size, mine, full, sem[2:4])
    wait_all(copies)
    total_ref[...] = slot_sum(slots, sizes["ctx"])


def first_kernel(
    sizes, part, tokens, fixed, up, down,
    full, out_ref, normed_ref, inverse_ref, wide_up, wide_down,
    slots, sums, *sem
):
    size, data = sizes["tensor"], sizes["dp"]
    mine = lax.axis_index("dp")
    greet_line(size, [pair_group(data)])
    line_start(size, part, slots, sem[0:2])
    place_up, place_down = (lambda index: wide_up.at[index]), (lambda index: wide_down.at[index])
    ups = gather_start(data, up, place_up, sem[4:10])
    downs = gather_start(data, down, place_down, sem[10:16])
    wide_up[mine] = up[...]
    wide_down[mine] = down[...]

    def finish(flow, k, total):
        first_sum = tokens[flow, k].astype(F32) + total + fixed[0:1]
        first_out, normed, inverse = layer_norm(first_sum, fixed[1:2], fixed[2:3])
        out_ref[k] = first_out
        normed_ref[k] = normed
        inverse_ref[k] = inverse
        return first_out.astype(BF16)

    line_run(size, part, slots, sums, full, sem[0:4], finish)
    ups = gather_pass(data, ups, place_up, sem[4:10])
    downs = gather_pass(data, downs, place_down, sem[10:16])
    wait_all(ups)
    wait_all(downs)


def add_row(vector_ref, index, value):
    vector_ref[index : index + 1] += jnp.sum(value, axis=0, keepdims=True)


def second_kernel(
    sizes, part, first_out, cotangent, fixed,
    full, output_ref, back_ref, vector_ref,
    slots, sums, *sem
):
    size = sizes["tensor"]
    greet_line(size, [])
    line_start(size, part, slots, sem[0:2])
    vector_ref[...] = jnp.zeros_like(vector_ref)

    def finish(flow, k, total):
        second_sum = first_out[k] + total + fixed[3:4]
        result, normed, inverse = layer_norm(second_sum, fixed[4:5], fixed[5:6])
        upstream = cotangent[flow, k].astype(F32)
        d_second = norm_back(upstream, normed, inverse, fixed[4:5])
        output_ref[k] = result.astype(BF16)
        back_ref[k] = d_second
        add_row(vector_ref, 0, upstream)
        add_row(vector_ref, 1, upstream * normed)
        add_row(vector_ref, 2, d_second)
        return d_second.astype(BF16)

    line_run(size, part, slots, sums, full, sem[0:4], finish)


def grads_start(size, grads, chip, sem):
    me, partner, _ = pair_roles(size)
    copy = remote(
        grads.at[:, lax.rem(partner, 2)], chip, sem[0].at[0], sem[1].at[0], {"dp": partner}
    )
    copy.start()
    return copy


def grads_far(size, copy, grads, chip, merged, slots, sem):
    me, _, far = pair_roles(size)
    copy.wait()
    merged[...] = (grads[:, lax.rem(me, 2)].astype(F32) + chip[...].astype(F32)).astype(BF16)
    copies = [
        remote(
            merged.at[lax.div(to, 2)], slots.at[lax.div(me, 2)], sem[2].at[step], sem[3].at[step], {"dp": to}
        )
        for step, (to, _) in enumerate(far)
    ]
    for moving in copies:
        moving.start()
    slots[lax.div(me, 2)] = merged[lax.div(me, 2)]
    return copies


def blocks_start(sizes, value, blocks, sem):
    me = lax.axis_index("ctx")
    blocks[me] = value
    return send_all(
        lambda other: (blocks.at[me], blocks.at[me]), peers_of("ctx", sizes["ctx"]), sem[0], sem[1]
    )


def third_kernel(
    sizes, part, d_second, normed_ref, inverse_ref, fixed, grads_a, grads_b,
    full, back_ref, vector_ref, block_a, block_b,
    slots, sums, chip_a, chip_b, merged_a, merged_b, far_a, far_b, *sem
):
    size, data = sizes["tensor"], sizes["dp"]
    greet_line(size, [pair_group(data)])
    line_start(size, part, slots, sem[0:2])
    near_a = grads_start(data, grads_a, chip_a, sem[4:8])
    near_b = grads_start(data, grads_b, chip_b, sem[8:12])
    vector_ref[...] = jnp.zeros_like(vector_ref)
    moving_a = grads_far(data, near_a, grads_a, chip_a, merged_a, far_a, sem[4:8])
    moving_b = grads_far(data, near_b, grads_b, chip_b, merged_b, far_b, sem[8:12])

    def finish(flow, k, total):
        d_first = total + d_second[k]
        normed = normed_ref[k]
        d_attn = norm_back(d_first, normed, inverse_ref[k], fixed[1:2])
        back_ref[k] = d_attn
        add_row(vector_ref, 0, d_first)
        add_row(vector_ref, 1, d_first * normed)
        add_row(vector_ref, 2, d_attn)
        return d_attn.astype(BF16)

    line_run(size, part, slots, sums, full, sem[0:4], finish)
    wait_all(moving_a)
    block_a[...] = slot_sum(far_a, data // 2).astype(BF16)
    wait_all(moving_b)
    block_b[...] = slot_sum(far_b, data // 2).astype(BF16)


def last_kernel(
    sizes, part, d_attn, grads, block_a, block_b, vectors,
    full, owned, owned_a, owned_b, vector_ref,
    slots, sums, chip, merged, far, blocks, blocks_a, blocks_b, slots_v, grid_v, *sem
):
    size, data = sizes["tensor"], sizes["dp"]
    me = lax.axis_index("tensor")
    rows = peers_of("tensor", size)
    here, everyone = grid_peers(sizes)
    greet([rows, everyone])
    line_start(size, part, slots, sem[0:2])
    small = send_all(lambda other: (vectors, slots_v.at[me]), rows, sem[8], sem[9])
    near = grads_start(data, grads, chip, sem[4:8])
    moving_a = blocks_start(sizes, block_a[...], blocks_a, sem[12:14])
    moving_b = blocks_start(sizes, block_b[...], blocks_b, sem[14:16])
    slots_v[me] = vectors[...]
    moving = grads_far(data, near, grads, chip, merged, far, sem[4:8])
    wait_all(small)
    own = vectors[...]
    row_ids = lax.broadcasted_iota(jnp.int32, own.shape, 0)
    grid_v[here] = jnp.where(row_ids < 6, slot_sum(slots_v, size), own)
    small = send_all(lambda other: (grid_v.at[here], grid_v.at[here]), everyone, sem[10], sem[11])

    def finish(flow, k, total):
        return (total + d_attn[k]).astype(BF16)

    line_run(size, part, slots, sums, full, sem[0:4], finish)
    wait_all(moving)
    moving = blocks_start(sizes, slot_sum(far, data // 2).astype(BF16), blocks, sem[16:18])
    wait_all(small)
    vector_ref[...] = slot_sum(grid_v, data * sizes["ctx"])
    wait_all(moving_a)
    owned_a[...] = slot_sum(blocks_a, sizes["ctx"])
    wait_all(moving_b)
    owned_b[...] = slot_sum(blocks_b, sizes["ctx"])
    wait_all(moving)
    owned[...] = slot_sum(blocks, sizes["ctx"])


CONTRACT_LAST = (((1,), (1,)), ((), ()))
CONTRACT_FIRST = (((0,), (0,)), ((), ()))


def forward_kernel(score_scale, length_ref, q_ref, k_ref, v_ref, out_ref, low_ref, log_ref):
    length = length_ref[0]
    rows, width = q_ref.shape
    keys = k_ref.shape[0]
    block = math.gcd(rows, 256)
    valid = lax.broadcasted_iota(jnp.int32, (block, keys), 1) < length

    @pl.loop(0, rows // block)
    def _(step):
        here = pl.ds(pl.multiple_of(step * block, block), block)
        for head in range(width // HD):
            lanes = slice(head * HD, (head + 1) * HD)
            scores = lax.dot_general(
                q_ref[here, lanes], k_ref[:, lanes], CONTRACT_LAST, preferred_element_type=F32
            ) * score_scale
            scores = jnp.where(valid, scores, NEGATIVE)
            top = jnp.max(scores, axis=-1, keepdims=True)
            weights = jnp.where(valid, jnp.exp(scores - top), 0.0)
            total = jnp.sum(weights, axis=-1, keepdims=True)
            acc = jnp.dot(weights.astype(BF16), v_ref[:, lanes], preferred_element_type=F32)
            attended = acc / total
            out_ref[here, lanes] = attended
            low_ref[here, lanes] = attended.astype(BF16)
            log_ref[here, head : head + 1] = top + jnp.log(total)


def backward_kernel(
    score_scale, length_ref, q_ref, k_ref, v_ref, heads_ref, attended_ref, log_ref,
    dq_ref, dk_ref, dv_ref
):
    length = length_ref[0]
    rows, width = q_ref.shape
    keys = k_ref.shape[0]
    block = math.gcd(rows, 256)
    valid = lax.broadcasted_iota(jnp.int32, (block, keys), 1) < length
    dk_ref[...] = jnp.zeros_like(dk_ref)
    dv_ref[...] = jnp.zeros_like(dv_ref)

    @pl.loop(0, rows // block)
    def _(step):
        here = pl.ds(pl.multiple_of(step * block, block), block)
        for head in range(width // HD):
            lanes = slice(head * HD, (head + 1) * HD)
            q, k, v, d_heads = q_ref[here, lanes], k_ref[:, lanes], v_ref[:, lanes], heads_ref[here, lanes]
            delta = jnp.sum(d_heads.astype(F32) * attended_ref[here, lanes], axis=-1, keepdims=True)
            scores = lax.dot_general(q, k, CONTRACT_LAST, preferred_element_type=F32) * score_scale
            scores = jnp.where(valid, scores, NEGATIVE)
            probs = jnp.where(valid, jnp.exp(scores - log_ref[here, head : head + 1]), 0.0)
            d_probs = lax.dot_general(d_heads, v, CONTRACT_LAST, preferred_element_type=F32)
            d_scores = (probs * (d_probs - delta)).astype(BF16)
            dv_ref[:, lanes] += lax.dot_general(
                probs.astype(BF16), d_heads, CONTRACT_FIRST, preferred_element_type=F32
            )
            dk_ref[:, lanes] += lax.dot_general(
                d_scores, q, CONTRACT_FIRST, preferred_element_type=F32
            ) * score_scale
            dq_ref[here, lanes] = jnp.dot(d_scores, k, preferred_element_type=F32) * score_scale


def attention_call(kernel, outs, args, name):
    return pl.pallas_call(
        kernel,
        out_shape=outs,
        in_specs=[pl.BlockSpec(memory_space=pltpu.SMEM)] + [VMEM_SPEC] * (len(args) - 1),
        out_specs=[VMEM_SPEC] * len(outs),
        compiler_params=pltpu.CompilerParams(vmem_limit_bytes=56 * 2**20),
        name=name,
    )(*args)


def per_device(
    sizes,
    tokens,
    lengths,
    cotangent,
    qkv_weight,
    query_bias,
    value_bias,
    proj_weight,
    proj_bias,
    first_gain,
    first_shift,
    up_weight,
    up_bias,
    down_weight,
    down_bias,
    second_gain,
    second_shift,
):
    data, blocks, ranks = sizes["dp"], sizes["ctx"], sizes["tensor"]
    rows_in = tokens[0]
    row_count, model = rows_in.shape
    half = row_count // 2
    chunk = math.gcd(half, 32)
    chunks = half // chunk
    piece, local_width = qkv_weight.shape[1:]
    up_width = up_weight.shape[1]
    score_scale = 1.0 / math.sqrt(HD)
    split = (2, chunks, chunk, model)
    line_scratch = [pltpu.VMEM(split, BF16)] * 2 + line_sems(chunks, 4)
    local = shaped(split[1:], F32)
    fixed = jnp.stack([proj_bias, first_gain, first_shift, down_bias, second_gain, second_shift])

    (wide_qkv,) = call(
        functools.partial(gather_kernel, sizes),
        [shaped((3, data, piece, local_width), BF16)],
        pair_sems(data),
        0,
        (qkv_weight,),
        "gather_weights",
    )
    wide_qkv = wide_qkv.reshape(3, model, local_width)

    projected = jnp.einsum("td,ide->ite", rows_in, wide_qkv, preferred_element_type=F32)
    queries = (projected[0] + query_bias).astype(BF16)
    own_kv = jnp.concatenate(
        [projected[1].astype(BF16), (projected[2] + value_bias).astype(BF16)], axis=1
    )
    kv, wide_proj = call(
        functools.partial(ctx_gather_kernel, sizes),
        [shaped((blocks,) + own_kv.shape, BF16), shaped((data,) + proj_weight.shape, BF16)],
        sems(blocks - 1) + pair_sems(data),
        1,
        (own_kv, proj_weight),
        "gather_keys",
    )
    wide_proj = wide_proj.transpose(1, 0, 2).reshape(local_width, model)
    kv = kv.reshape(blocks * row_count, 2 * local_width)
    keys, values = kv[:, :local_width], kv[:, local_width:]
    attended, attended_low, log_total = attention_call(
        functools.partial(forward_kernel, score_scale),
        [
            shaped((row_count, local_width), F32),
            shaped((row_count, local_width), BF16),
            shaped((row_count, local_width // HD), F32),
        ],
        (lengths, queries, keys, values),
        "attention_forward",
    )
    attn_part = jnp.dot(attended_low, wide_proj, preferred_element_type=F32).astype(BF16)

    first_low, first_out, first_normed, first_inverse, wide_up, wide_down = call(
        functools.partial(first_kernel, sizes),
        [
            shaped(split, BF16),
            local,
            local,
            shaped((chunks, chunk, 1), F32),
            shaped((data,) + up_weight.shape, BF16),
            shaped((data,) + down_weight.shape, BF16),
        ],
        line_scratch + pair_sems(data) * 2,
        2,
        (
            attn_part.reshape(split),
            rows_in.reshape(split),
            fixed,
            up_weight,
            down_weight,
        ),
        "first_norm",
    )
    first_low = first_low.reshape(row_count, model)
    wide_up = wide_up.reshape(model, up_width)
    wide_down = wide_down.transpose(1, 0, 2).reshape(up_width, model)

    pre_act = jnp.dot(first_low, wide_up, preferred_element_type=F32) + up_bias
    hidden = gelu_value(pre_act).astype(BF16)
    down_part = jnp.dot(hidden, wide_down, preferred_element_type=F32).astype(BF16)
    d_second_low, output_part, d_second, second_vectors = call(
        functools.partial(second_kernel, sizes),
        [shaped(split, BF16), shaped(split[1:], BF16), local, shaped((3, model), F32)],
        line_scratch,
        3,
        (
            down_part.reshape(split),
            first_out,
            cotangent[0].reshape(split),
            fixed,
        ),
        "second_norm",
    )
    d_second_low = d_second_low.reshape(row_count, model)
    grad_down = jnp.einsum("td,tf->df", d_second_low, hidden, preferred_element_type=F32)
    d_hidden = jnp.einsum("td,fd->tf", d_second_low, wide_down, preferred_element_type=F32)
    d_pre = d_hidden * gelu_slope(pre_act)
    grad_up_bias = jnp.sum(d_pre, axis=0)
    d_pre_low = d_pre.astype(BF16)
    grad_up = jnp.einsum("td,tf->df", first_low, d_pre_low, preferred_element_type=F32)
    first_part = jnp.einsum("tf,df->td", d_pre_low, wide_up, preferred_element_type=F32).astype(BF16)

    grad_shape = (data, model // data, up_width)
    paired = (data // 2, 2) + grad_shape[1:]
    pair_slots = pltpu.VMEM((data // 2,) + grad_shape[1:], BF16)
    pair_moves = sems(1) + sems(max(1, data // 2 - 1))
    d_attn_low, d_attn, first_vectors, block_up, block_down = call(
        functools.partial(third_kernel, sizes),
        [shaped(split, BF16), local, shaped((3, model), F32)] + [shaped(grad_shape[1:], BF16)] * 2,
        line_scratch[:2] + [pair_slots] * 6 + line_scratch[2:] + pair_moves * 2,
        4,
        (
            first_part.reshape(split),
            d_second,
            first_normed,
            first_inverse,
            fixed,
            grad_up.astype(BF16).reshape(paired),
            grad_down.astype(BF16).reshape(paired),
        ),
        "first_norm_back",
    )
    d_attn_low = d_attn_low.reshape(row_count, model)
    d_heads = jnp.einsum("td,ed->te", d_attn_low, wide_proj, preferred_element_type=F32).astype(BF16)
    d_query, key_grads, value_grads = attention_call(
        functools.partial(backward_kernel, score_scale),
        [shaped((row_count, local_width), F32)]
        + [shaped((blocks * row_count, local_width), F32)] * 2,
        (lengths, queries, keys, values, d_heads, attended, log_total),
        "attention_backward",
    )
    kv_part = jnp.concatenate([key_grads.astype(BF16), value_grads.astype(BF16)], axis=1)
    kv_shape = (blocks, row_count, 2 * local_width)
    own_grads, output = call(
        functools.partial(ctx_sum_kernel, sizes),
        [shaped(kv_shape[1:], F32), shaped(split, BF16)],
        [pltpu.VMEM(kv_shape, BF16)] + sems(blocks - 1) + line_sems(chunks, 2),
        5,
        (kv_part.reshape(kv_shape), output_part),
        "sum_keys",
    )
    grad_query_bias = jnp.sum(d_query, axis=0)
    grad_value_bias = jnp.sum(own_grads[:, local_width:], axis=0)
    d_stack = jnp.concatenate([d_query.astype(BF16), own_grads.astype(BF16)], axis=1)
    grad_qkv = jnp.einsum("td,te->de", rows_in, d_stack, preferred_element_type=F32)
    grad_proj = jnp.einsum("td,te->de", d_attn_low, attended_low, preferred_element_type=F32)
    flat_qkv = wide_qkv.transpose(1, 0, 2).reshape(model, 3 * local_width)
    input_part = jnp.einsum("te,de->td", d_stack, flat_qkv, preferred_element_type=F32).astype(BF16)

    last_shape = (data // 2, 2, model // data, 4 * local_width)
    last_pair = pltpu.VMEM((data // 2,) + last_shape[2:], BF16)
    last_grads = jnp.concatenate([grad_qkv.astype(BF16), grad_proj.astype(BF16)], axis=1)
    vector_width = max(model, up_width, 2 * local_width)
    pad = lambda array: jnp.pad(array, ((0, 0), (0, vector_width - array.shape[1])))
    vectors = jnp.concatenate(
        [
            pad(second_vectors),
            pad(first_vectors),
            pad(grad_up_bias[None]),
            pad(jnp.concatenate([grad_query_bias, grad_value_bias])[None]),
        ]
    )
    grad_tokens, own_last, own_up, own_down, sums = call(
        functools.partial(last_kernel, sizes),
        [shaped(split, BF16), shaped(last_shape[2:], F32)]
        + [shaped(grad_shape[1:], F32)] * 2
        + [shaped(vectors.shape, F32)],
        line_scratch[:2]
        + [last_pair] * 3
        + [pltpu.VMEM((blocks,) + last_shape[2:], BF16)]
        + [pltpu.VMEM((blocks,) + grad_shape[1:], BF16)] * 2
        + [
            pltpu.VMEM((ranks,) + vectors.shape, F32),
            pltpu.VMEM((data * blocks,) + vectors.shape, F32),
        ]
        + line_scratch[2:]
        + pair_moves
        + sems(ranks - 1)
        + sems(data * blocks - 1)
        + sems(blocks - 1) * 3,
        6,
        (
            input_part.reshape(split),
            d_attn,
            last_grads.reshape(last_shape),
            block_up,
            block_down,
            vectors,
        ),
        "token_grads",
    )
    grad_tokens = grad_tokens.reshape(1, row_count, model).astype(F32)
    own_qkv = own_last[:, : 3 * local_width].reshape(-1, 3, local_width).transpose(1, 0, 2)
    return (
        output.reshape(1, row_count, model),
        grad_tokens,
        own_qkv,
        sums[7, :local_width],
        sums[7, local_width : 2 * local_width],
        own_last[:, 3 * local_width :].T,
        sums[5, :model],
        sums[4, :model],
        sums[3, :model],
        own_up,
        sums[6, :up_width],
        own_down.T,
        sums[2, :model],
        sums[1, :model],
        sums[0, :model],
    )


def solution(mesh):
    placed = (
        P("dp", "ctx", None),
        P("dp"),
        P("dp", "ctx", None),
        P(None, "dp", "tensor"),
        P("tensor"),
        P("tensor"),
        P("tensor", "dp"),
        P(),
        P(),
        P(),
        P("dp", "tensor"),
        P("tensor"),
        P("tensor", "dp"),
        P(),
        P(),
        P(),
    )
    return jax.shard_map(
        functools.partial(per_device, dict(mesh.shape)),
        mesh=mesh,
        in_specs=placed,
        out_specs=(
            P("dp", "ctx", None),
            P("dp", "ctx", None),
            P(None, "dp", "tensor"),
            P("tensor"),
            P("tensor"),
            P("tensor", "dp"),
            P(),
            P(),
            P(),
            P("dp", "tensor"),
            P("tensor"),
            P("tensor", "dp"),
            P(),
            P(),
            P(),
        ),
        check_vma=False,
    )
```
